32 devices in a mesh: groups: 2 (over x), ep: 16 (over z, y, core).
Axes of the slice: x: 2, y: 2, z: 4, core: 2. Of those that a mesh axis runs over, the one named last changes fastest.
Arguments:
- residual: bfloat16 [512, 2048], P(('groups', 'ep')), parts along dimension 0, may hold values from -54 to 54
- norm_gain: bfloat16 [2048], replicated, may hold values from 0.099609375 to 1.8984375
- expert_ids: int32 [512, 8], P(('groups', 'ep')), parts along dimension 0, may hold values from 0 to 15, as said below
- route_weights: float32 [512, 8], P(('groups', 'ep')), parts along dimension 0, may hold values from 0.05 to 1
- w_gate: bfloat16 [16, 2, 2048, 384], P('ep'), may hold values from -0.125 to 0.125
- w_up: bfloat16 [16, 2, 2048, 384], P('ep'), may hold values from -0.125 to 0.125
- w_down: bfloat16 [16, 2, 384, 2048], P('ep'), may hold values from -0.21875 to 0.21875
Outputs:
- layer_out: bfloat16 [512, 2048], P(('groups', 'ep')), parts along dimension 0
The draws below stay inside these ranges and needn't reach their ends.
There are 2 independent parts, one for each index of `groups`. The reference program is written for one: setup_inputs(seed, part) draws one part's arguments, and reference() takes and returns one part's arrays. A program takes and returns all parts, laid end to end along the dimension named above; an argument that names none is the same for every part. Nothing has to cross between parts.
Inputs may be any that keep to these rules, and one draw needn't show every extreme that they name: `expert_ids`: each row names 8 different experts. Among the rows of one device no expert is named by more than 16 rows, and no pair of experts 2 j and 2 j + 1 by more than 16 rows (a row that names both counts once); each bound is reached on some device.
All inputs are finite; a program needn't handle non-finite values.
Results may differ from the reference program's by a relative error of at most 0.004.
Values may be sent and summed in bfloat16 or wider, within the bound.
No kernel may reach another device: no remote copies, remote signals or barrier semaphores. Data moves between devices by JAX's collectives and lax.ppermute only.
A program may use at most 64 MiB of HBM per device.

```python
import math
import jax
import jax.numpy as jnp
from jax import lax

D = 2048
FF = 768
TOP = 8
REQ_DEV = 16
EXPERTS = 16
REQ = 256
CAP = 16
BCAP = 16
N_EP = 16


def draw_residual(key, part):
    values = jax.random.truncated_normal(jax.random.fold_in(key, 31), -6.0, 6.0, (REQ, D), jnp.float32)
    return values.astype(jnp.bfloat16)


def draw_expert_ids(key, part):
    block_total = EXPERTS // 2
    ranking = jax.random.permutation(jax.random.fold_in(key, 21), EXPERTS).astype(jnp.int32)
    standing = jnp.zeros((EXPERTS,), jnp.int32).at[ranking].set(jnp.arange(EXPERTS, dtype=jnp.int32))
    frequent_experts = 24 * (standing < max(1, EXPERTS // 8)).astype(jnp.int32) + 24 * (standing < max(1, EXPERTS // 32)).astype(jnp.int32)
    heaviest_expert = ranking[0]
    offset_block = jax.random.randint(jax.random.fold_in(key, 22), (), 1, block_total)
    last_block = block_total - 1
    planted = jnp.where(heaviest_expert // 2 == last_block, (heaviest_expert // 2 + offset_block) % block_total, last_block).astype(jnp.int32)
    random_noise = jax.random.randint(jax.random.fold_in(key, 23), (N_EP, REQ_DEV, EXPERTS), 0, 64)
    expert_pool = jnp.arange(EXPERTS, dtype=jnp.int32)
    row_index = jnp.arange(REQ_DEV, dtype=jnp.int32)
    favored_expert_boost = jnp.where(expert_pool == heaviest_expert, 1000, 0)
    inserted_choice = 2 * planted + row_index % 2
    inserted_expert_boost = jnp.where(expert_pool[None, :] == inserted_choice[:, None], 900, 0)
    router_logits = random_noise + frequent_experts[None, None, :] + favored_expert_boost[None, None, :] + inserted_expert_boost[None, :, :]
    ordered = (router_logits * EXPERTS + expert_pool[None, None, :]).astype(jnp.int32)

    def one_device(device_scores):

        def one_row(carry_state, row_scores):
            counts, block_counts = carry_state
            allowed = jnp.logical_and(counts < CAP, jnp.repeat(block_counts, 2) < BCAP)
            masked = jnp.where(allowed, row_scores, -1)
            chosen = lax.top_k(masked, TOP)[1].astype(jnp.int32)
            onehot = (chosen[:, None] == expert_pool[None, :]).astype(jnp.int32)
            taken_now = jnp.sum(onehot, axis=0)
            counts = counts + taken_now
            block_counts = block_counts + (jnp.sum(taken_now.reshape(block_total, 2), axis=1) > 0).astype(jnp.int32)
            return ((counts, block_counts), chosen)
        start_state = (jnp.zeros((EXPERTS,), jnp.int32), jnp.zeros((block_total,), jnp.int32))
        return lax.scan(one_row, start_state, device_scores)[1]
    routes = jax.vmap(one_device)(ordered)
    return routes.reshape(REQ, TOP).astype(jnp.int32)


def levels(stream_key, dims, shards, smallest, largest):
    loudness, own = 1.0, jax.random.fold_in(stream_key, 6)
    for position, shards_of in shards:
        steps = jnp.exp(jax.random.uniform(jax.random.fold_in(own, position), (shards_of,), jnp.float32, smallest / len(shards), largest / len(shards)))
        loudness = loudness * jnp.repeat(steps, dims[position] // shards_of).reshape([-1 if axis == position else 1 for axis in range(len(dims))])
    return loudness


def normal_values(own_key, shape, spread, reach, split=(), kind=jnp.bfloat16):
    factor_of = levels(own_key, shape, split, -0.22, 0.18) if split else 1.0
    values = jax.random.normal(own_key, shape, jnp.float32) * spread * factor_of
    return jnp.minimum(jnp.maximum(values, -reach), reach).astype(kind)


def setup_inputs(seed: int = 0, part: int = 0) -> dict:
    streams_of = jax.random.split(jax.random.key(seed), 8)
    part_splits = jax.random.split(jax.random.fold_in(streams_of[7], part), 8)
    return {
        "residual": draw_residual(jax.random.fold_in(jax.random.fold_in(streams_of[7], part), 71), part),
        "norm_gain": jnp.clip(1.0 + 0.18 * jax.random.normal(streams_of[1], (D,), jnp.float32), 0.099609375, 1.8984375).astype(jnp.bfloat16),
        "expert_ids": draw_expert_ids(jax.random.fold_in(jax.random.fold_in(streams_of[7], part), 71), part),
        "route_weights": jnp.clip(jnp.exp(math.log(1.0) - 2.9957323 * jax.random.uniform(part_splits[3], (REQ, TOP), jnp.float32) ** levels(part_splits[3], (REQ, TOP), ((0, 16),), -0.2, 0.2)), 0.05, 1.0),
        "w_gate": normal_values(streams_of[4], (EXPERTS, 2, D, FF // 2), D ** -0.5, 0.125, ((0, 16),)),
        "w_up": normal_values(streams_of[5], (EXPERTS, 2, D, FF // 2), D ** -0.5, 0.125, ((0, 16),)),
        "w_down": normal_values(streams_of[6], (EXPERTS, 2, FF // 2, D), FF ** -0.5, 0.21875, ((0, 16),)),
    }


def reference(residual, norm_gain, expert_ids, route_weights, w_gate, w_up, w_down):
    widened = residual.astype(jnp.float32)
    scaling = lax.rsqrt(lax.optimization_barrier(jnp.mean(widened * widened, axis=1, keepdims=True)) + 1e-06)
    normed = (widened * scaling * norm_gain.astype(jnp.float32)[None, :]).astype(jnp.bfloat16)
    shares = (route_weights / lax.optimization_barrier(jnp.sum(route_weights, axis=1, keepdims=True))).astype(jnp.bfloat16)
    flat_ids = expert_ids.reshape(-1)
    flat_shares = shares.reshape(-1).astype(jnp.float32)
    row_count = residual.shape[0]
    bound_rows = N_EP * CAP

    def one_expert(combined, expert_index):
        chosen = flat_ids == expert_index
        picked = jnp.nonzero(chosen, size=bound_rows, fill_value=0)[0].astype(jnp.int32)
        filled = jnp.arange(bound_rows, dtype=jnp.int32) < jnp.sum(chosen.astype(jnp.int32))
        selected = normed[picked // TOP]
        first_slot = 2 * (expert_index // 2)
        member = expert_index % 2
        gate_mat = jnp.concatenate([w_gate[first_slot, member], w_gate[first_slot + 1, member]], axis=1)
        up_mat = jnp.concatenate([w_up[first_slot, member], w_up[first_slot + 1, member]], axis=1)
        down_mat = jnp.concatenate([w_down[first_slot, member], w_down[first_slot + 1, member]], axis=0)
        gate_part = jnp.dot(selected, gate_mat, preferred_element_type=jnp.float32)
        upper = jnp.dot(selected, up_mat, preferred_element_type=jnp.float32)
        inner = (jax.nn.silu(gate_part) * upper).astype(jnp.bfloat16)
        answer = jnp.dot(inner, down_mat, preferred_element_type=jnp.float32)
        weight = jnp.where(filled, flat_shares[picked], jnp.zeros((), jnp.float32))
        targets = jnp.where(filled, picked // TOP, row_count)
        return (combined.at[targets].add(weight[:, None] * answer, mode='drop'), expert_index)
    combined = lax.scan(one_expert, jnp.zeros((row_count, D), jnp.float32), jnp.arange(EXPERTS, dtype=jnp.int32))[0]
    return (widened + combined).astype(jnp.bfloat16)
```

```python
import jax
import jax.numpy as jnp
from jax import lax
from jax.experimental import pallas as pl
from jax.experimental.pallas import tpu as pltpu
from jax.sharding import PartitionSpec as P

TOP = 8
LANES = 128
BF16 = jnp.bfloat16
F32 = jnp.float32


def exchanged(value, axis, mask):
    pairs = [(source, source ^ mask) for source in range(lax.axis_size(axis))]
    return lax.ppermute(value, axis, pairs)


def swapped(value, axis, distance):
    return exchanged(value, axis, 2**distance)


def message_kernel(residual_ref, gain_ref, ids_ref, routes_ref, out_ref):
    rows, width = residual_ref.shape
    widened = residual_ref[...].astype(F32)
    scaling = lax.rsqrt(jnp.mean(widened * widened, axis=1, keepdims=True) + 1e-06)
    normed = widened * scaling * gain_ref[...].astype(F32)
    out_ref[:, :width] = normed.astype(BF16)
    routes = routes_ref[...]
    shares = (routes / jnp.sum(routes, axis=0, keepdims=True)).astype(BF16).astype(F32)
    experts = lax.broadcasted_iota(jnp.int32, (LANES, rows), 0)
    table = jnp.zeros((LANES, rows), F32)
    for choice in range(routes.shape[0]):
        hit = ids_ref[choice : choice + 1, :] == experts
        table = table + jnp.where(hit, shares[choice : choice + 1, :], 0.0)
    identity = (
        lax.broadcasted_iota(jnp.int32, (rows, rows), 0)
        == lax.broadcasted_iota(jnp.int32, (rows, rows), 1)
    ).astype(BF16)
    by_row = lax.dot_general(
        identity, table.astype(BF16), (((1,), (1,)), ((), ())), preferred_element_type=F32
    )
    out_ref[:, width:] = by_row.astype(BF16)


def outgoing_message(residual, norm_gain, expert_ids, route_weights):
    rows, width = residual.shape
    vmem = pl.BlockSpec(memory_space=pltpu.VMEM)
    return pl.pallas_call(
        message_kernel,
        out_shape=jax.ShapeDtypeStruct((rows, width + LANES), BF16),
        in_specs=[vmem] * 4,
        out_specs=vmem,
        name="message",
    )(residual, norm_gain.reshape(1, width), expert_ids.T, route_weights.T)


def expert_kernel(first_ref, *refs):
    half = (len(refs) - 5) // 2
    own, sibling = refs[:half], refs[half : 2 * half]
    gate_ref, up_ref, down_ref, kept_ref, sent_ref = refs[2 * half :]
    width = gate_ref.shape[2]
    hidden = gate_ref.shape[3]
    even = hidden // 256 * 256
    rest = hidden - even
    rows = jnp.concatenate([ref[:, :width] for ref in own + sibling], axis=0)
    table = jnp.concatenate([ref[:, width:] for ref in own + sibling], axis=0).astype(F32)
    lanes = lax.broadcasted_iota(jnp.int32, table.shape, 1)
    inners = []
    for member in range(2):
        share = jnp.sum(
            jnp.where(lanes == first_ref[0] + member, table, 0.0), axis=1, keepdims=True
        )
        gate_mat, up_mat = gate_ref[0, member], up_ref[0, member]
        gate = jnp.dot(rows, gate_mat[:, :even], preferred_element_type=F32)
        upper = jnp.dot(rows, up_mat[:, :even], preferred_element_type=F32)
        if rest:
            both = jnp.concatenate([gate_mat[:, even:], up_mat[:, even:]], axis=1)
            last = jnp.dot(rows, both, preferred_element_type=F32)
            gate = jnp.concatenate([gate, last[:, :rest]], axis=1)
            upper = jnp.concatenate([upper, last[:, rest:]], axis=1)
        inners.append((gate * jax.nn.sigmoid(gate) * upper * share).astype(BF16))
    inner = jnp.concatenate(inners, axis=1)
    down = jnp.concatenate([down_ref[0, 0], down_ref[0, 1]], axis=0)
    answer = jnp.dot(inner, down, preferred_element_type=F32)
    split = kept_ref.shape[0]
    kept_ref[...] = answer[:split]
    sent_ref[...] = answer[split:].astype(BF16)


def expert_sums(first, own, sibling, w_gate, w_up, w_down):
    local_rows = own[0].shape[0]
    width = w_down.shape[3]
    rows = local_rows * len(own)
    vmem = pl.BlockSpec(memory_space=pltpu.VMEM)
    smem = pl.BlockSpec(memory_space=pltpu.SMEM)
    weight_count = 2 * 3 * w_down.shape[2] * width
    return pl.pallas_call(
        expert_kernel,
        out_shape=(
            jax.ShapeDtypeStruct((rows, width), F32),
            jax.ShapeDtypeStruct((rows, width), BF16),
        ),
        in_specs=[smem] + [vmem] * (2 * len(own) + 3),
        out_specs=(vmem, vmem),
        compiler_params=pltpu.CompilerParams(vmem_limit_bytes=24 * 2**20),
        cost_estimate=pl.CostEstimate(
            flops=2 * 2 * rows * weight_count,
            bytes_accessed=2 * weight_count,
            transcendentals=0,
        ),
        name="experts",
    )(first, *own, *sibling, w_gate, w_up, w_down)


def dense(residual, norm_gain, expert_ids, route_weights, w_gate, w_up, w_down):
    rows = residual.shape[0]
    far = lax.axis_size("ep") // 2
    left, near, both = far // 2, far // 4, far // 2 + far // 4
    first = (lax.axis_index("ep") // 2 * 2).reshape(1)

    def to(value, mask):
        return exchanged(value, "ep", mask)

    block = {0: outgoing_message(residual, norm_gain, expert_ids, route_weights)}
    block[far] = to(block[0], far)
    block[near] = to(block[0], near)
    block[left] = to(block[0], left)
    block[both] = to(block[0], both)
    block[far + left] = to(block[far], left)
    block[far + near] = to(block[far], near)
    block[far + both] = to(block[far], both)
    sibling = {mask: to(value, 1) for mask, value in block.items()}

    def sums(masks):
        kept, sent = expert_sums(
            first,
            [block[mask] for mask in masks],
            [sibling[mask] for mask in masks],
            w_gate,
            w_up,
            w_down,
        )
        total = kept + to(sent, 1).astype(F32)
        return {mask: total[i * rows : (i + 1) * rows] for i, mask in enumerate(masks)}

    sum_of = sums((0, near, left, both))
    sum_of.update(sums((far, far + near, far + left, far + both)))

    relayed = to(
        jnp.concatenate([sum_of[both], sum_of[far + left]], axis=0).astype(BF16), left
    ).astype(F32)
    from_near = to(sum_of[far + near].astype(BF16), near).astype(F32)
    from_both = to(sum_of[far + both].astype(BF16), both).astype(F32)
    from_left = to(sum_of[left].astype(BF16), left).astype(F32)
    for_near = to((sum_of[near] + relayed[:rows]).astype(BF16), near).astype(F32)
    for_far = to(
        (sum_of[far] + relayed[rows:] + from_near + from_both).astype(BF16), far
    ).astype(F32)
    combined = sum_of[0] + from_left + for_near + for_far
    return (residual.astype(F32) + combined).astype(BF16)


def half_ffn(inputs, gate_mat, up_mat, down_mat):
    gate_part = jnp.dot(inputs, gate_mat, preferred_element_type=jnp.float32)
    upper = jnp.dot(inputs, up_mat, preferred_element_type=jnp.float32)
    inner = (jax.nn.silu(gate_part) * upper).astype(jnp.bfloat16)
    return jnp.dot(inner, down_mat, preferred_element_type=jnp.float32)


def pair_tables(expert_ids, shares, normed, block_total, slot_total):
    local_rows = normed.shape[0]
    expert_total = 2 * block_total
    block_iota = lax.broadcasted_iota(jnp.int32, (1, 1, block_total), 2)
    block_hits = jnp.any((expert_ids // 2)[:, :, None] == block_iota, axis=1).astype(jnp.int32)
    block_rank = jnp.cumsum(block_hits, axis=0) - 1
    hit_wide = jnp.repeat(block_hits, slot_total, axis=1)
    rank_wide = jnp.repeat(block_rank, slot_total, axis=1)
    slot_place = lax.broadcasted_iota(jnp.int32, (1, block_total * slot_total), 1) % slot_total
    picker = jnp.logical_and(hit_wide > 0, rank_wide == slot_place)
    expert_iota = lax.broadcasted_iota(jnp.int32, (1, 1, expert_total), 2)
    expert_mask = expert_ids[:, :, None] == expert_iota
    share_table = jnp.sum(
        jnp.where(expert_mask, shares[:, :, None], jnp.zeros((), jnp.bfloat16)), axis=1
    )
    share_wide = jnp.repeat(share_table.reshape(local_rows, block_total, 2), slot_total, axis=1)
    slot_weights = jnp.sum(
        jnp.where(picker[:, :, None], share_wide, jnp.zeros((), jnp.bfloat16)), axis=0
    )
    slot_rows = jnp.einsum(
        "rs,rd->sd", picker.astype(jnp.bfloat16), normed, preferred_element_type=jnp.float32
    ).astype(jnp.bfloat16)
    return (picker, slot_rows, slot_weights)


def sparse(residual, norm_gain, expert_ids, route_weights, w_gate, w_up, w_down):
    local_rows = residual.shape[0]
    model_width = residual.shape[1]
    widened = residual.astype(jnp.float32)
    scaling = lax.rsqrt(jnp.mean(widened * widened, axis=1, keepdims=True) + 1e-06)
    normed = (widened * scaling * norm_gain.astype(jnp.float32)[None, :]).astype(jnp.bfloat16)
    shares = (route_weights / jnp.sum(route_weights, axis=1, keepdims=True)).astype(jnp.bfloat16)
    device_total = lax.axis_size("ep")
    block_total = device_total // 2
    typical = max(1, local_rows * TOP // device_total)

    def weighted_both(arrived, arrived_weights):
        flat_rows = arrived.reshape(-1, arrived.shape[2])
        flat_weights = arrived_weights.reshape(-1, 2).astype(jnp.float32)
        mixed = flat_weights[:, 0:1] * half_ffn(flat_rows, w_gate[0, 0], w_up[0, 0], w_down[0, 0])
        mixed = mixed + flat_weights[:, 1:2] * half_ffn(
            flat_rows, w_gate[0, 1], w_up[0, 1], w_down[0, 1]
        )
        return mixed.reshape(arrived.shape)

    pair_slots = min(local_rows, 4 * typical)
    half_slots = (pair_slots + 1) // 2
    padded_slots = 2 * half_slots
    picker, slot_rows, slot_weights = pair_tables(
        expert_ids, shares, normed, block_total, padded_slots
    )
    outgoing = slot_rows.reshape(device_total, half_slots, model_width)
    weights_out = slot_weights.reshape(device_total, half_slots, 2)
    arrived = lax.all_to_all(outgoing, "ep", split_axis=0, concat_axis=0, tiled=True)
    arrived_weights = lax.all_to_all(weights_out, "ep", split_axis=0, concat_axis=0, tiled=True)
    other_rows, other_weights = swapped((arrived, arrived_weights), "ep", 0)
    mine = weighted_both(arrived, arrived_weights)
    theirs = weighted_both(other_rows, other_weights)
    back = swapped(theirs, "ep", 0)
    answered = mine + back
    returned = lax.all_to_all(answered, "ep", split_axis=0, concat_axis=0, tiled=True)
    pooled = returned.reshape(block_total * padded_slots, model_width)
    combined = jnp.dot(picker.astype(jnp.float32), pooled, precision=lax.Precision.HIGHEST)
    return (widened + combined).astype(jnp.bfloat16)


def local(*args):
    devices = lax.axis_size("ep")
    if devices == 2 * TOP:
        return dense(*args)
    return sparse(*args)


def solution(mesh):
    placed = (
        P(("groups", "ep"), None),
        P(),
        P(("groups", "ep"), None),
        P(("groups", "ep"), None),
        P("ep", None, None, None),
        P("ep", None, None, None),
        P("ep", None, None, None),
    )
    return jax.shard_map(
        local, mesh=mesh, in_specs=placed, out_specs=P(("groups", "ep"), None), check_vma=False
    )
```

```python
import jax
import jax.numpy as jnp
from jax import lax
from jax.experimental import pallas as pl
from jax.experimental.pallas import tpu as pltpu
from jax.sharding import PartitionSpec as P


TOP = 8
LANES = 128
BF16 = jnp.bfloat16
F32 = jnp.float32


def exchanged(value, axis, mask):
    pairs = [(source, source ^ mask) for source in range(lax.axis_size(axis))]
    return lax.ppermute(value, axis, pairs)


def swapped(value, axis, distance):
    return exchanged(value, axis, 2**distance)


def message_kernel(residual_ref, gain_ref, ids_ref, routes_ref, out_ref):
    rows, width = residual_ref.shape
    widened = residual_ref[...].astype(F32)
    scaling = lax.rsqrt(jnp.mean(widened * widened, axis=1, keepdims=True) + 1e-06)
    scaled = widened * scaling
    for piece in range(gain_ref.shape[0]):
        lanes = slice(piece * LANES, (piece + 1) * LANES)
        gain = gain_ref[piece : piece + 1, :].astype(F32)
        out_ref[:, lanes] = (scaled[:, lanes] * gain).astype(BF16)
    routes = routes_ref[...]
    shares = (routes / jnp.sum(routes, axis=0, keepdims=True)).astype(BF16).astype(F32)
    experts = lax.broadcasted_iota(jnp.int32, (LANES, rows), 0)
    table = jnp.zeros((LANES, rows), F32)
    for choice in range(routes.shape[0]):
        hit = ids_ref[choice : choice + 1, :] == experts
        table = table + jnp.where(hit, shares[choice : choice + 1, :], 0.0)
    identity = (
        lax.broadcasted_iota(jnp.int32, (rows, rows), 0)
        == lax.broadcasted_iota(jnp.int32, (rows, rows), 1)
    ).astype(BF16)
    by_row = lax.dot_general(
        identity, table.astype(BF16), (((1,), (1,)), ((), ())), preferred_element_type=F32
    )
    out_ref[:, width:] = by_row.astype(BF16)


def outgoing_message(residual, norm_gain, expert_ids, route_weights):
    rows, width = residual.shape
    vmem = pl.BlockSpec(memory_space=pltpu.VMEM)
    return pl.pallas_call(
        message_kernel,
        out_shape=jax.ShapeDtypeStruct((rows, width + LANES), BF16),
        in_specs=[vmem] * 4,
        out_specs=vmem,
        compiler_params=pltpu.CompilerParams(vmem_limit_bytes=2**25),
        name="message",
    )(residual, norm_gain.reshape(width // LANES, LANES), expert_ids.T, route_weights.T)


def gap_kernel(out_ref):
    out_ref[0] = 0


def gap():
    return pl.pallas_call(
        gap_kernel,
        out_shape=jax.ShapeDtypeStruct((1,), jnp.int32),
        out_specs=pl.BlockSpec(memory_space=pltpu.SMEM),
        compiler_params=pltpu.CompilerParams(vmem_limit_bytes=2**20, has_side_effects=True),
        cost_estimate=pl.CostEstimate(flops=20 * 10**9, bytes_accessed=2**20, transcendentals=0),
        name="gap",
    )()


def expert_kernel(*refs):
    first = lax.axis_index("ep") & -2
    half = (len(refs) - 5) // 2
    own, sibling = refs[:half], refs[half : 2 * half]
    gate_ref, up_ref, down_ref, kept_ref, sent_ref = refs[2 * half :]
    width = gate_ref.shape[2]
    hidden = gate_ref.shape[3]
    even = hidden // 256 * 256
    rest = hidden - even
    rows = jnp.concatenate([ref[:, :width] for ref in own + sibling], axis=0)
    table = jnp.concatenate([ref[:, width:] for ref in own + sibling], axis=0).astype(F32)
    lanes = lax.broadcasted_iota(jnp.int32, table.shape, 1)
    inners = []
    for member in range(2):
        share = jnp.sum(
            jnp.where(lanes == first + member, table, 0.0), axis=1, keepdims=True
        )
        gate_mat, up_mat = gate_ref[0, member], up_ref[0, member]
        gate = jnp.dot(rows, gate_mat[:, :even], preferred_element_type=F32)
        upper = jnp.dot(rows, up_mat[:, :even], preferred_element_type=F32)
        if rest:
            both = jnp.concatenate([gate_mat[:, even:], up_mat[:, even:]], axis=1)
            last = jnp.dot(rows, both, preferred_element_type=F32)
            gate = jnp.concatenate([gate, last[:, :rest]], axis=1)
            upper = jnp.concatenate([upper, last[:, rest:]], axis=1)
        inners.append((gate * jax.nn.sigmoid(gate) * upper * share).astype(BF16))
    inner = jnp.concatenate(inners, axis=1)
    down = jnp.concatenate([down_ref[0, 0], down_ref[0, 1]], axis=0)
    answer = jnp.dot(inner, down, preferred_element_type=F32)
    split = kept_ref.shape[0]
    kept_ref[...] = answer[:split]
    sent_ref[...] = answer[split:].astype(BF16)


def expert_sums(own, sibling, w_gate, w_up, w_down):
    local_rows = own[0].shape[0]
    width = w_down.shape[3]
    rows = local_rows * len(own)
    vmem = pl.BlockSpec(memory_space=pltpu.VMEM)
    weight_count = 2 * 3 * w_down.shape[2] * width
    return pl.pallas_call(
        expert_kernel,
        out_shape=(
            jax.ShapeDtypeStruct((rows, width), F32),
            jax.ShapeDtypeStruct((rows, width), BF16),
        ),
        in_specs=[vmem] * (2 * len(own) + 3),
        out_specs=(vmem, vmem),
        compiler_params=pltpu.CompilerParams(vmem_limit_bytes=24 * 2**20),
        cost_estimate=pl.CostEstimate(
            flops=2 * 2 * rows * weight_count,
            bytes_accessed=2 * weight_count,
            transcendentals=0,
        ),
        name="experts",
    )(*own, *sibling, w_gate, w_up, w_down)


def dense(residual, norm_gain, expert_ids, route_weights, w_gate, w_up, w_down):
    rows = residual.shape[0]
    far = lax.axis_size("ep") // 2
    left, near, both = far // 2, far // 4, far // 2 + far // 4
    quarter = (0, near, left, both)

    def to(value, mask):
        return exchanged(value, "ep", mask)

    def widened(value, mask):
        return to(value.astype(BF16), mask).astype(F32)

    block = {0: outgoing_message(residual, norm_gain, expert_ids, route_weights)}
    gap()
    block[far] = to(block[0], far)
    block[left] = to(block[0], left)
    block[near] = to(block[0], near)
    block[both] = to(block[0], both)
    block[far + both] = to(block[far], both)
    block[far + left] = to(block[far], left)
    block[far + near] = to(block[far], near)

    def answers(masks):
        sibling = [to(block[mask], 1) for mask in masks]
        kept, sent = expert_sums(
            [block[mask] for mask in masks], sibling, w_gate, w_up, w_down
        )
        return kept, to(sent, 1)

    def split(kept, back, masks):
        total = kept + back.astype(F32)
        return {mask: total[i * rows : (i + 1) * rows] for i, mask in enumerate(masks)}

    kept_a, back_a = answers(quarter)
    kept_b, back_b = answers([far + mask for mask in quarter])
    kept_a, kept_b, back_a, back_b = lax.optimization_barrier((kept_a, kept_b, back_a, back_b))
    sum_of = split(kept_a, back_a, quarter)
    sum_of.update(split(kept_b, back_b, [far + mask for mask in quarter]))

    from_both = widened(sum_of[far + both], both)
    relayed = widened(jnp.concatenate([sum_of[both], sum_of[far + left]], axis=0), left)
    from_near = widened(sum_of[far + near], near)
    from_far = widened(sum_of[far] + relayed[rows:] + from_near + from_both, far)
    for_near = widened(sum_of[near] + relayed[:rows], near)
    from_left = widened(sum_of[left], left)
    combined = sum_of[0] + from_left + for_near + from_far
    return (residual.astype(F32) + combined).astype(BF16)


def half_ffn(inputs, gate_mat, up_mat, down_mat):
    gate_part = jnp.dot(inputs, gate_mat, preferred_element_type=jnp.float32)
    upper = jnp.dot(inputs, up_mat, preferred_element_type=jnp.float32)
    inner = (jax.nn.silu(gate_part) * upper).astype(jnp.bfloat16)
    return jnp.dot(inner, down_mat, preferred_element_type=jnp.float32)


def pair_tables(expert_ids, shares, normed, block_total, slot_total):
    local_rows = normed.shape[0]
    expert_total = 2 * block_total
    block_iota = lax.broadcasted_iota(jnp.int32, (1, 1, block_total), 2)
    block_hits = jnp.any((expert_ids // 2)[:, :, None] == block_iota, axis=1).astype(jnp.int32)
    block_rank = jnp.cumsum(block_hits, axis=0) - 1
    hit_wide = jnp.repeat(block_hits, slot_total, axis=1)
    rank_wide = jnp.repeat(block_rank, slot_total, axis=1)
    slot_place = lax.broadcasted_iota(jnp.int32, (1, block_total * slot_total), 1) % slot_total
    picker = jnp.logical_and(hit_wide > 0, rank_wide == slot_place)
    expert_iota = lax.broadcasted_iota(jnp.int32, (1, 1, expert_total), 2)
    expert_mask = expert_ids[:, :, None] == expert_iota
    share_table = jnp.sum(
        jnp.where(expert_mask, shares[:, :, None], jnp.zeros((), jnp.bfloat16)), axis=1
    )
    share_wide = jnp.repeat(share_table.reshape(local_rows, block_total, 2), slot_total, axis=1)
    slot_weights = jnp.sum(
        jnp.where(picker[:, :, None], share_wide, jnp.zeros((), jnp.bfloat16)), axis=0
    )
    slot_rows = jnp.einsum(
        "rs,rd->sd", picker.astype(jnp.bfloat16), normed, preferred_element_type=jnp.float32
    ).astype(jnp.bfloat16)
    return (picker, slot_rows, slot_weights)


def sparse(residual, norm_gain, expert_ids, route_weights, w_gate, w_up, w_down):
    local_rows = residual.shape[0]
    model_width = residual.shape[1]
    widened = residual.astype(jnp.float32)
    scaling = lax.rsqrt(jnp.mean(widened * widened, axis=1, keepdims=True) + 1e-06)
    normed = (widened * scaling * norm_gain.astype(jnp.float32)[None, :]).astype(jnp.bfloat16)
    shares = (route_weights / jnp.sum(route_weights, axis=1, keepdims=True)).astype(jnp.bfloat16)
    device_total = lax.axis_size("ep")
    block_total = device_total // 2
    typical = max(1, local_rows * TOP // device_total)

    def weighted_both(arrived, arrived_weights):
        flat_rows = arrived.reshape(-1, arrived.shape[2])
        flat_weights = arrived_weights.reshape(-1, 2).astype(jnp.float32)
        mixed = flat_weights[:, 0:1] * half_ffn(flat_rows, w_gate[0, 0], w_up[0, 0], w_down[0, 0])
        mixed = mixed + flat_weights[:, 1:2] * half_ffn(
            flat_rows, w_gate[0, 1], w_up[0, 1], w_down[0, 1]
        )
        return mixed.reshape(arrived.shape)

    pair_slots = min(local_rows, 4 * typical)
    half_slots = (pair_slots + 1) // 2
    padded_slots = 2 * half_slots
    picker, slot_rows, slot_weights = pair_tables(
        expert_ids, shares, normed, block_total, padded_slots
    )
    outgoing = slot_rows.reshape(device_total, half_slots, model_width)
    weights_out = slot_weights.reshape(device_total, half_slots, 2)
    arrived = lax.all_to_all(outgoing, "ep", split_axis=0, concat_axis=0, tiled=True)
    arrived_weights = lax.all_to_all(weights_out, "ep", split_axis=0, concat_axis=0, tiled=True)
    other_rows, other_weights = swapped((arrived, arrived_weights), "ep", 0)
    mine = weighted_both(arrived, arrived_weights)
    theirs = weighted_both(other_rows, other_weights)
    back = swapped(theirs, "ep", 0)
    answered = mine + back
    returned = lax.all_to_all(answered, "ep", split_axis=0, concat_axis=0, tiled=True)
    pooled = returned.reshape(block_total * padded_slots, model_width)
    combined = jnp.dot(picker.astype(jnp.float32), pooled, precision=lax.Precision.HIGHEST)
    return (widened + combined).astype(jnp.bfloat16)


def few_experts(devices):
    return devices == 2 * TOP


def local(*args):
    return (dense if few_experts(lax.axis_size("ep")) else sparse)(*args)


def solution(mesh):
    placed = (
        P(("groups", "ep"), None),
        P(),
        P(("groups", "ep"), None),
        P(("groups", "ep"), None),
        P("ep", None, None, None),
        P("ep", None, None, None),
        P("ep", None, None, None),
    )
    return jax.shard_map(
        local, mesh=mesh, in_specs=placed, out_specs=P(("groups", "ep"), None), check_vma=False
    )
```

```python
import jax
import jax.numpy as jnp
from jax import lax
from jax.experimental import pallas as pl
from jax.experimental.pallas import tpu as pltpu
from jax.sharding import PartitionSpec as P


TOP = 8
LANES = 128
BF16 = jnp.bfloat16
F32 = jnp.float32


def exchanged(value, axis, mask):
    pairs = [(source, source ^ mask) for source in range(lax.axis_size(axis))]
    return lax.ppermute(value, axis, pairs)


def swapped(value, axis, distance):
    return exchanged(value, axis, 2**distance)


def message_kernel(residual_ref, gain_ref, ids_ref, routes_ref, out_ref):
    rows, width = residual_ref.shape
    widened = residual_ref[...].astype(F32)
    scaling = lax.rsqrt(jnp.mean(widened * widened, axis=1, keepdims=True) + 1e-06)
    scaled = widened * scaling
    for piece in range(gain_ref.shape[0]):
        lanes = slice(piece * LANES, (piece + 1) * LANES)
        gain = gain_ref[piece : piece + 1, :].astype(F32)
        out_ref[:, lanes] = (scaled[:, lanes] * gain).astype(BF16)
    routes = routes_ref[...]
    shares = (routes / jnp.sum(routes, axis=0, keepdims=True)).astype(BF16).astype(F32)
    experts = lax.broadcasted_iota(jnp.int32, (LANES, rows), 0)
    table = jnp.zeros((LANES, rows), F32)
    for choice in range(routes.shape[0]):
        hit = ids_ref[choice : choice + 1, :] == experts
        table = table + jnp.where(hit, shares[choice : choice + 1, :], 0.0)
    identity = (
        lax.broadcasted_iota(jnp.int32, (rows, rows), 0)
        == lax.broadcasted_iota(jnp.int32, (rows, rows), 1)
    ).astype(BF16)
    by_row = lax.dot_general(
        identity, table.astype(BF16), (((1,), (1,)), ((), ())), preferred_element_type=F32
    )
    out_ref[:, width:] = by_row.astype(BF16)


def outgoing_message(residual, norm_gain, expert_ids, route_weights):
    rows, width = residual.shape
    vmem = pl.BlockSpec(memory_space=pltpu.VMEM)
    return pl.pallas_call(
        message_kernel,
        out_shape=jax.ShapeDtypeStruct((rows, width + LANES), BF16),
        in_specs=[vmem] * 4,
        out_specs=vmem,
        compiler_params=pltpu.CompilerParams(vmem_limit_bytes=2**25),
        name="message",
    )(residual, norm_gain.reshape(width // LANES, LANES), expert_ids.T, route_weights.T)


def gap_kernel(out_ref):
    out_ref[0] = 0


def gap():
    return pl.pallas_call(
        gap_kernel,
        out_shape=jax.ShapeDtypeStruct((1,), jnp.int32),
        out_specs=pl.BlockSpec(memory_space=pltpu.SMEM),
        compiler_params=pltpu.CompilerParams(vmem_limit_bytes=2**20, has_side_effects=True),
        cost_estimate=pl.CostEstimate(flops=20 * 10**9, bytes_accessed=2**20, transcendentals=0),
        name="gap",
    )()


def expert_kernel(*refs):
    first = lax.axis_index("ep") & -2
    half = (len(refs) - 5) // 2
    own, sibling = refs[:half], refs[half : 2 * half]
    gate_ref, up_ref, down_ref, kept_ref, sent_ref = refs[2 * half :]
    width = gate_ref.shape[2]
    hidden = gate_ref.shape[3]
    even = hidden // 256 * 256
    rest = hidden - even
    rows = jnp.concatenate([ref[:, :width] for ref in own + sibling], axis=0)
    table = jnp.concatenate([ref[:, width:] for ref in own + sibling], axis=0).astype(F32)
    lanes = lax.broadcasted_iota(jnp.int32, table.shape, 1)
    inners = []
    for member in range(2):
        share = jnp.sum(
            jnp.where(lanes == first + member, table, 0.0), axis=1, keepdims=True
        )
        gate_mat, up_mat = gate_ref[0, member], up_ref[0, member]
        gate = jnp.dot(rows, gate_mat[:, :even], preferred_element_type=F32)
        upper = jnp.dot(rows, up_mat[:, :even], preferred_element_type=F32)
        if rest:
            both = jnp.concatenate([gate_mat[:, even:], up_mat[:, even:]], axis=1)
            last = jnp.dot(rows, both, preferred_element_type=F32)
            gate = jnp.concatenate([gate, last[:, :rest]], axis=1)
            upper = jnp.concatenate([upper, last[:, rest:]], axis=1)
        inners.append((gate * jax.nn.sigmoid(gate) * upper * share).astype(BF16))
    inner = jnp.concatenate(inners, axis=1)
    down = jnp.concatenate([down_ref[0, 0], down_ref[0, 1]], axis=0)
    answer = jnp.dot(inner, down, preferred_element_type=F32)
    split = kept_ref.shape[0]
    kept_ref[...] = answer[:split]
    sent_ref[...] = answer[split:].astype(BF16)


def expert_sums(own, sibling, w_gate, w_up, w_down):
    local_rows = own[0].shape[0]
    width = w_down.shape[3]
    rows = local_rows * len(own)
    vmem = pl.BlockSpec(memory_space=pltpu.VMEM)
    weight_count = 2 * 3 * w_down.shape[2] * width
    return pl.pallas_call(
        expert_kernel,
        out_shape=(
            jax.ShapeDtypeStruct((rows, width), F32),
            jax.ShapeDtypeStruct((rows, width), BF16),
        ),
        in_specs=[vmem] * (2 * len(own) + 3),
        out_specs=(vmem, vmem),
        compiler_params=pltpu.CompilerParams(vmem_limit_bytes=24 * 2**20),
        cost_estimate=pl.CostEstimate(
            flops=2 * 2 * rows * weight_count,
            bytes_accessed=2 * weight_count,
            transcendentals=0,
        ),
        name="experts",
    )(*own, *sibling, w_gate, w_up, w_down)


def dense(residual, norm_gain, expert_ids, route_weights, w_gate, w_up, w_down):
    rows = residual.shape[0]
    far = lax.axis_size("ep") // 2
    left, near, both = far // 2, far // 4, far // 2 + far // 4

    def to(value, mask):
        return exchanged(value, "ep", mask)

    def widened(value, mask):
        return to(value.astype(BF16), mask).astype(F32)

    gap()
    own = outgoing_message(residual, norm_gain, expert_ids, route_weights)
    from_far = to(own, far)
    from_left = to(own, left)
    near_half = {"own": own, "left": from_left, "near": to(own, near), "both": to(from_left, near)}
    far_half = {
        "own": from_far,
        "both": to(from_far, both),
        "left": to(from_far, left),
        "near": to(from_far, near),
    }

    def answers(blocks):
        sibling = [to(block, 1) for block in blocks.values()]
        kept, sent = expert_sums(list(blocks.values()), sibling, w_gate, w_up, w_down)
        return kept, to(sent, 1)

    def split(kept, back, names):
        total = kept + back.astype(F32)
        return {name: total[i * rows : (i + 1) * rows] for i, name in enumerate(names)}

    kept_far, back_far = answers(far_half)
    kept_near, back_near = answers(near_half)
    kept_far, back_far, kept_near = lax.optimization_barrier((kept_far, back_far, kept_near))
    for_far = split(kept_far, back_far, far_half)
    for_near = split(kept_near, back_near, near_half)

    by_both = widened(for_far["both"], both)
    by_left = widened(for_far["left"], left)
    by_near = widened(for_far["near"], near)
    folded = widened(for_near["both"], left)
    across = widened(for_far["own"] + by_left + by_near + by_both, far)
    beside = widened(for_near["left"], left)
    below = widened(for_near["near"] + folded, near)
    combined = for_near["own"] + beside + below + across
    return (residual.astype(F32) + combined).astype(BF16)


def half_ffn(inputs, gate_mat, up_mat, down_mat):
    gate_part = jnp.dot(inputs, gate_mat, preferred_element_type=jnp.float32)
    upper = jnp.dot(inputs, up_mat, preferred_element_type=jnp.float32)
    inner = (jax.nn.silu(gate_part) * upper).astype(jnp.bfloat16)
    return jnp.dot(inner, down_mat, preferred_element_type=jnp.float32)


def pair_tables(expert_ids, shares, normed, block_total, slot_total):
    local_rows = normed.shape[0]
    expert_total = 2 * block_total
    block_iota = lax.broadcasted_iota(jnp.int32, (1, 1, block_total), 2)
    block_hits = jnp.any((expert_ids // 2)[:, :, None] == block_iota, axis=1).astype(jnp.int32)
    block_rank = jnp.cumsum(block_hits, axis=0) - 1
    hit_wide = jnp.repeat(block_hits, slot_total, axis=1)
    rank_wide = jnp.repeat(block_rank, slot_total, axis=1)
    slot_place = lax.broadcasted_iota(jnp.int32, (1, block_total * slot_total), 1) % slot_total
    picker = jnp.logical_and(hit_wide > 0, rank_wide == slot_place)
    expert_iota = lax.broadcasted_iota(jnp.int32, (1, 1, expert_total), 2)
    expert_mask = expert_ids[:, :, None] == expert_iota
    share_table = jnp.sum(
        jnp.where(expert_mask, shares[:, :, None], jnp.zeros((), jnp.bfloat16)), axis=1
    )
    share_wide = jnp.repeat(share_table.reshape(local_rows, block_total, 2), slot_total, axis=1)
    slot_weights = jnp.sum(
        jnp.where(picker[:, :, None], share_wide, jnp.zeros((), jnp.bfloat16)), axis=0
    )
    slot_rows = jnp.einsum(
        "rs,rd->sd", picker.astype(jnp.bfloat16), normed, preferred_element_type=jnp.float32
    ).astype(jnp.bfloat16)
    return (picker, slot_rows, slot_weights)


def sparse(residual, norm_gain, expert_ids, route_weights, w_gate, w_up, w_down):
    local_rows = residual.shape[0]
    model_width = residual.shape[1]
    widened = residual.astype(jnp.float32)
    scaling = lax.rsqrt(jnp.mean(widened * widened, axis=1, keepdims=True) + 1e-06)
    normed = (widened * scaling * norm_gain.astype(jnp.float32)[None, :]).astype(jnp.bfloat16)
    shares = (route_weights / jnp.sum(route_weights, axis=1, keepdims=True)).astype(jnp.bfloat16)
    device_total = lax.axis_size("ep")
    block_total = device_total // 2
    typical = max(1, local_rows * TOP // device_total)

    def weighted_both(arrived, arrived_weights):
        flat_rows = arrived.reshape(-1, arrived.shape[2])
        flat_weights = arrived_weights.reshape(-1, 2).astype(jnp.float32)
        mixed = flat_weights[:, 0:1] * half_ffn(flat_rows, w_gate[0, 0], w_up[0, 0], w_down[0, 0])
        mixed = mixed + flat_weights[:, 1:2] * half_ffn(
            flat_rows, w_gate[0, 1], w_up[0, 1], w_down[0, 1]
        )
        return mixed.reshape(arrived.shape)

    pair_slots = min(local_rows, 4 * typical)
    half_slots = (pair_slots + 1) // 2
    padded_slots = 2 * half_slots
    picker, slot_rows, slot_weights = pair_tables(
        expert_ids, shares, normed, block_total, padded_slots
    )
    outgoing = slot_rows.reshape(device_total, half_slots, model_width)
    weights_out = slot_weights.reshape(device_total, half_slots, 2)
    arrived = lax.all_to_all(outgoing, "ep", split_axis=0, concat_axis=0, tiled=True)
    arrived_weights = lax.all_to_all(weights_out, "ep", split_axis=0, concat_axis=0, tiled=True)
    other_rows, other_weights = swapped((arrived, arrived_weights), "ep", 0)
    mine = weighted_both(arrived, arrived_weights)
    theirs = weighted_both(other_rows, other_weights)
    back = swapped(theirs, "ep", 0)
    answered = mine + back
    returned = lax.all_to_all(answered, "ep", split_axis=0, concat_axis=0, tiled=True)
    pooled = returned.reshape(block_total * padded_slots, model_width)
    combined = jnp.dot(picker.astype(jnp.float32), pooled, precision=lax.Precision.HIGHEST)
    return (widened + combined).astype(jnp.bfloat16)


def few_experts(devices):
    return devices == 2 * TOP


def local(*args):
    return (dense if few_experts(lax.axis_size("ep")) else sparse)(*args)


def solution(mesh):
    placed = (
        P(("groups", "ep"), None),
        P(),
        P(("groups", "ep"), None),
        P(("groups", "ep"), None),
        P("ep", None, None, None),
        P("ep", None, None, None),
        P("ep", None, None, None),
    )
    return jax.shard_map(
        local, mesh=mesh, in_specs=placed, out_specs=P(("groups", "ep"), None), check_vma=False
    )
```

```python
import jax
import jax.numpy as jnp
from jax import lax
from jax.experimental import pallas as pl
from jax.experimental.pallas import tpu as pltpu
from jax.sharding import PartitionSpec as P


TOP = 8
LANES = 128
BF16 = jnp.bfloat16
F32 = jnp.float32


def exchanged(value, axis, mask):
    pairs = [(source, source ^ mask) for source in range(lax.axis_size(axis))]
    return lax.ppermute(value, axis, pairs)


def swapped(value, axis, distance):
    return exchanged(value, axis, 2**distance)


def message_kernel(residual_ref, gain_ref, ids_ref, routes_ref, out_ref):
    rows, width = residual_ref.shape
    widened = residual_ref[...].astype(F32)
    scaling = lax.rsqrt(jnp.mean(widened * widened, axis=1, keepdims=True) + 1e-06)
    scaled = widened * scaling
    for piece in range(gain_ref.shape[0]):
        lanes = slice(piece * LANES, (piece + 1) * LANES)
        gain = gain_ref[piece : piece + 1, :].astype(F32)
        out_ref[:, lanes] = (scaled[:, lanes] * gain).astype(BF16)
    routes = routes_ref[...]
    shares = (routes / jnp.sum(routes, axis=0, keepdims=True)).astype(BF16).astype(F32)
    experts = lax.broadcasted_iota(jnp.int32, (LANES, rows), 0)
    table = jnp.zeros((LANES, rows), F32)
    for choice in range(routes.shape[0]):
        hit = ids_ref[choice : choice + 1, :] == experts
        table = table + jnp.where(hit, shares[choice : choice + 1, :], 0.0)
    identity = (
        lax.broadcasted_iota(jnp.int32, (rows, rows), 0)
        == lax.broadcasted_iota(jnp.int32, (rows, rows), 1)
    ).astype(BF16)
    by_row = lax.dot_general(
        identity, table.astype(BF16), (((1,), (1,)), ((), ())), preferred_element_type=F32
    )
    out_ref[:, width:] = by_row.astype(BF16)


def outgoing_message(residual, norm_gain, expert_ids, route_weights):
    rows, width = residual.shape
    vmem = pl.BlockSpec(memory_space=pltpu.VMEM)
    return pl.pallas_call(
        message_kernel,
        out_shape=jax.ShapeDtypeStruct((rows, width + LANES), BF16),
        in_specs=[vmem] * 4,
        out_specs=vmem,
        compiler_params=pltpu.CompilerParams(vmem_limit_bytes=2**25),
        name="message",
    )(residual, norm_gain.reshape(width // LANES, LANES), expert_ids.T, route_weights.T)


def gap_kernel(out_ref):
    out_ref[0] = 0


def gap():
    return pl.pallas_call(
        gap_kernel,
        out_shape=jax.ShapeDtypeStruct((1,), jnp.int32),
        out_specs=pl.BlockSpec(memory_space=pltpu.SMEM),
        compiler_params=pltpu.CompilerParams(vmem_limit_bytes=2**20, has_side_effects=True),
        cost_estimate=pl.CostEstimate(flops=20 * 10**9, bytes_accessed=2**20, transcendentals=0),
        name="gap",
    )()


def expert_kernel(*refs):
    first = lax.axis_index("ep") & -2
    half = (len(refs) - 5) // 2
    own, sibling = refs[:half], refs[half : 2 * half]
    gate_ref, up_ref, down_ref, kept_ref, sent_ref = refs[2 * half :]
    width = gate_ref.shape[2]
    hidden = gate_ref.shape[3]
    even = hidden // 256 * 256
    rest = hidden - even
    rows = jnp.concatenate([ref[:, :width] for ref in own + sibling], axis=0)
    table = jnp.concatenate([ref[:, width:] for ref in own + sibling], axis=0).astype(F32)
    lanes = lax.broadcasted_iota(jnp.int32, table.shape, 1)
    inners = []
    for member in range(2):
        share = jnp.sum(
            jnp.where(lanes == first + member, table, 0.0), axis=1, keepdims=True
        )
        gate_mat, up_mat = gate_ref[0, member], up_ref[0, member]
        gate = jnp.dot(rows, gate_mat[:, :even], preferred_element_type=F32)
        upper = jnp.dot(rows, up_mat[:, :even], preferred_element_type=F32)
        if rest:
            both = jnp.concatenate([gate_mat[:, even:], up_mat[:, even:]], axis=1)
            last = jnp.dot(rows, both, preferred_element_type=F32)
            gate = jnp.concatenate([gate, last[:, :rest]], axis=1)
            upper = jnp.concatenate([upper, last[:, rest:]], axis=1)
        inners.append((gate * jax.nn.sigmoid(gate) * upper * share).astype(BF16))
    inner = jnp.concatenate(inners, axis=1)
    down = jnp.concatenate([down_ref[0, 0], down_ref[0, 1]], axis=0)
    answer = jnp.dot(inner, down, preferred_element_type=F32)
    split = kept_ref.shape[0]
    kept_ref[...] = answer[:split]
    sent_ref[...] = answer[split:].astype(BF16)


def expert_sums(own, sibling, w_gate, w_up, w_down):
    local_rows = own[0].shape[0]
    width = w_down.shape[3]
    rows = local_rows * len(own)
    vmem = pl.BlockSpec(memory_space=pltpu.VMEM)
    weight_count = 2 * 3 * w_down.shape[2] * width
    return pl.pallas_call(
        expert_kernel,
        out_shape=(
            jax.ShapeDtypeStruct((rows, width), F32),
            jax.ShapeDtypeStruct((rows, width), BF16),
        ),
        in_specs=[vmem] * (2 * len(own) + 3),
        out_specs=(vmem, vmem),
        compiler_params=pltpu.CompilerParams(vmem_limit_bytes=24 * 2**20),
        cost_estimate=pl.CostEstimate(
            flops=2 * 2 * rows * weight_count,
            bytes_accessed=2 * weight_count,
            transcendentals=0,
        ),
        name="experts",
    )(*own, *sibling, w_gate, w_up, w_down)


def dense(residual, norm_gain, expert_ids, route_weights, w_gate, w_up, w_down):
    rows = residual.shape[0]
    far = lax.axis_size("ep") // 2
    left, near, both = far // 2, far // 4, far // 2 + far // 4

    def to(value, mask):
        return exchanged(value, "ep", mask)

    def widened(value, mask):
        return to(value.astype(BF16), mask).astype(F32)

    gap()
    own = outgoing_message(residual, norm_gain, expert_ids, route_weights)
    from_far = to(own, far)
    from_left = to(own, left)
    early = {
        "own": own,
        "left": from_left,
        "near": to(own, near),
        "far": from_far,
    }
    late = {
        "far_both": to(from_far, both),
        "far_left": to(from_far, left),
        "far_near": to(from_far, near),
        "both": to(own, both),
    }

    def answers(blocks):
        sibling = [to(block, 1) for block in blocks.values()]
        kept, sent = expert_sums(list(blocks.values()), sibling, w_gate, w_up, w_down)
        return kept, to(sent, 1)

    def split(kept, back, names):
        total = kept + back.astype(F32)
        return {name: total[i * rows : (i + 1) * rows] for i, name in enumerate(names)}

    kept_early, back_early = answers(early)
    kept_late, back_late = answers(late)
    kept_early, back_early, kept_late = lax.optimization_barrier(
        (kept_early, back_early, kept_late)
    )
    total = split(kept_early, back_early, early)
    total.update(split(kept_late, back_late, late))

    beside = widened(total["left"], left)
    by_both = widened(total["far_both"], both)
    by_left = widened(total["far_left"], left)
    by_near = widened(total["far_near"], near)
    below = widened(total["near"], near)
    across = widened(total["both"], both)
    opposite = widened(total["far"] + by_left + by_near + by_both, far)
    combined = total["own"] + beside + below + across + opposite
    return (residual.astype(F32) + combined).astype(BF16)


def half_ffn(inputs, gate_mat, up_mat, down_mat):
    gate_part = jnp.dot(inputs, gate_mat, preferred_element_type=jnp.float32)
    upper = jnp.dot(inputs, up_mat, preferred_element_type=jnp.float32)
    inner = (jax.nn.silu(gate_part) * upper).astype(jnp.bfloat16)
    return jnp.dot(inner, down_mat, preferred_element_type=jnp.float32)


def pair_tables(expert_ids, shares, normed, block_total, slot_total):
    local_rows = normed.shape[0]
    expert_total = 2 * block_total
    block_iota = lax.broadcasted_iota(jnp.int32, (1, 1, block_total), 2)
    block_hits = jnp.any((expert_ids // 2)[:, :, None] == block_iota, axis=1).astype(jnp.int32)
    block_rank = jnp.cumsum(block_hits, axis=0) - 1
    hit_wide = jnp.repeat(block_hits, slot_total, axis=1)
    rank_wide = jnp.repeat(block_rank, slot_total, axis=1)
    slot_place = lax.broadcasted_iota(jnp.int32, (1, block_total * slot_total), 1) % slot_total
    picker = jnp.logical_and(hit_wide > 0, rank_wide == slot_place)
    expert_iota = lax.broadcasted_iota(jnp.int32, (1, 1, expert_total), 2)
    expert_mask = expert_ids[:, :, None] == expert_iota
    share_table = jnp.sum(
        jnp.where(expert_mask, shares[:, :, None], jnp.zeros((), jnp.bfloat16)), axis=1
    )
    share_wide = jnp.repeat(share_table.reshape(local_rows, block_total, 2), slot_total, axis=1)
    slot_weights = jnp.sum(
        jnp.where(picker[:, :, None], share_wide, jnp.zeros((), jnp.bfloat16)), axis=0
    )
    slot_rows = jnp.einsum(
        "rs,rd->sd", picker.astype(jnp.bfloat16), normed, preferred_element_type=jnp.float32
    ).astype(jnp.bfloat16)
    return (picker, slot_rows, slot_weights)


def sparse(residual, norm_gain, expert_ids, route_weights, w_gate, w_up, w_down):
    local_rows = residual.shape[0]
    model_width = residual.shape[1]
    widened = residual.astype(jnp.float32)
    scaling = lax.rsqrt(jnp.mean(widened * widened, axis=1, keepdims=True) + 1e-06)
    normed = (widened * scaling * norm_gain.astype(jnp.float32)[None, :]).astype(jnp.bfloat16)
    shares = (route_weights / jnp.sum(route_weights, axis=1, keepdims=True)).astype(jnp.bfloat16)
    device_total = lax.axis_size("ep")
    block_total = device_total // 2
    typical = max(1, local_rows * TOP // device_total)

    def weighted_both(arrived, arrived_weights):
        flat_rows = arrived.reshape(-1, arrived.shape[2])
        flat_weights = arrived_weights.reshape(-1, 2).astype(jnp.float32)
        mixed = flat_weights[:, 0:1] * half_ffn(flat_rows, w_gate[0, 0], w_up[0, 0], w_down[0, 0])
        mixed = mixed + flat_weights[:, 1:2] * half_ffn(
            flat_rows, w_gate[0, 1], w_up[0, 1], w_down[0, 1]
        )
        return mixed.reshape(arrived.shape)

    pair_slots = min(local_rows, 4 * typical)
    half_slots = (pair_slots + 1) // 2
    padded_slots = 2 * half_slots
    picker, slot_rows, slot_weights = pair_tables(
        expert_ids, shares, normed, block_total, padded_slots
    )
    outgoing = slot_rows.reshape(device_total, half_slots, model_width)
    weights_out = slot_weights.reshape(device_total, half_slots, 2)
    arrived = lax.all_to_all(outgoing, "ep", split_axis=0, concat_axis=0, tiled=True)
    arrived_weights = lax.all_to_all(weights_out, "ep", split_axis=0, concat_axis=0, tiled=True)
    other_rows, other_weights = swapped((arrived, arrived_weights), "ep", 0)
    mine = weighted_both(arrived, arrived_weights)
    theirs = weighted_both(other_rows, other_weights)
    back = swapped(theirs, "ep", 0)
    answered = mine + back
    returned = lax.all_to_all(answered, "ep", split_axis=0, concat_axis=0, tiled=True)
    pooled = returned.reshape(block_total * padded_slots, model_width)
    combined = jnp.dot(picker.astype(jnp.float32), pooled, precision=lax.Precision.HIGHEST)
    return (widened + combined).astype(jnp.bfloat16)


def few_experts(devices):
    return devices == 2 * TOP


def local(*args):
    return (dense if few_experts(lax.axis_size("ep")) else sparse)(*args)


def solution(mesh):
    placed = (
        P(("groups", "ep"), None),
        P(),
        P(("groups", "ep"), None),
        P(("groups", "ep"), None),
        P("ep", None, None, None),
        P("ep", None, None, None),
        P("ep", None, None, None),
    )
    return jax.shard_map(
        local, mesh=mesh, in_specs=placed, out_specs=P(("groups", "ep"), None), check_vma=False
    )
```

```python
import jax
import jax.numpy as jnp
from jax import lax
from jax.experimental import pallas as pl
from jax.experimental.pallas import tpu as pltpu
from jax.sharding import PartitionSpec as P


TOP = 8
LANES = 128
BF16 = jnp.bfloat16
F32 = jnp.float32


def exchanged(value, axis, mask):
    pairs = [(source, source ^ mask) for source in range(lax.axis_size(axis))]
    return lax.ppermute(value, axis, pairs)


def swapped(value, axis, distance):
    return exchanged(value, axis, 2**distance)


def message_kernel(residual_ref, gain_ref, ids_ref, routes_ref, out_ref):
    rows, width = residual_ref.shape
    widened = residual_ref[...].astype(F32)
    scaling = lax.rsqrt(jnp.mean(widened * widened, axis=1, keepdims=True) + 1e-06)
    scaled = widened * scaling
    for piece in range(gain_ref.shape[0]):
        lanes = slice(piece * LANES, (piece + 1) * LANES)
        gain = gain_ref[piece : piece + 1, :].astype(F32)
        out_ref[:, lanes] = (scaled[:, lanes] * gain).astype(BF16)
    routes = routes_ref[...]
    shares = (routes / jnp.sum(routes, axis=0, keepdims=True)).astype(BF16).astype(F32)
    experts = lax.broadcasted_iota(jnp.int32, (LANES, rows), 0)
    table = jnp.zeros((LANES, rows), F32)
    for choice in range(routes.shape[0]):
        hit = ids_ref[choice : choice + 1, :] == experts
        table = table + jnp.where(hit, shares[choice : choice + 1, :], 0.0)
    identity = (
        lax.broadcasted_iota(jnp.int32, (rows, rows), 0)
        == lax.broadcasted_iota(jnp.int32, (rows, rows), 1)
    ).astype(BF16)
    by_row = lax.dot_general(
        identity, table.astype(BF16), (((1,), (1,)), ((), ())), preferred_element_type=F32
    )
    out_ref[:, width:] = by_row.astype(BF16)


def outgoing_message(residual, norm_gain, expert_ids, route_weights):
    rows, width = residual.shape
    vmem = pl.BlockSpec(memory_space=pltpu.VMEM)
    return pl.pallas_call(
        message_kernel,
        out_shape=jax.ShapeDtypeStruct((rows, width + LANES), BF16),
        in_specs=[vmem] * 4,
        out_specs=vmem,
        compiler_params=pltpu.CompilerParams(vmem_limit_bytes=2**25),
        name="message",
    )(residual, norm_gain.reshape(width // LANES, LANES), expert_ids.T, route_weights.T)


def gap_kernel(out_ref):
    out_ref[0] = 0


def gap():
    return pl.pallas_call(
        gap_kernel,
        out_shape=jax.ShapeDtypeStruct((1,), jnp.int32),
        out_specs=pl.BlockSpec(memory_space=pltpu.SMEM),
        compiler_params=pltpu.CompilerParams(vmem_limit_bytes=2**20, has_side_effects=True),
        cost_estimate=pl.CostEstimate(flops=20 * 10**9, bytes_accessed=2**20, transcendentals=0),
        name="gap",
    )()


def expert_kernel(*refs):
    first = lax.axis_index("ep") & -2
    half = (len(refs) - 5) // 2
    own, sibling = refs[:half], refs[half : 2 * half]
    gate_ref, up_ref, down_ref, kept_ref, sent_ref = refs[2 * half :]
    width = gate_ref.shape[2]
    hidden = gate_ref.shape[3]
    even = hidden // 256 * 256
    rest = hidden - even
    rows = jnp.concatenate([ref[:, :width] for ref in own + sibling], axis=0)
    table = jnp.concatenate([ref[:, width:] for ref in own + sibling], axis=0).astype(F32)
    lanes = lax.broadcasted_iota(jnp.int32, table.shape, 1)
    inners = []
    for member in range(2):
        share = jnp.sum(
            jnp.where(lanes == first + member, table, 0.0), axis=1, keepdims=True
        )
        gate_mat, up_mat = gate_ref[0, member], up_ref[0, member]
        gate = jnp.dot(rows, gate_mat[:, :even], preferred_element_type=F32)
        upper = jnp.dot(rows, up_mat[:, :even], preferred_element_type=F32)
        if rest:
            both = jnp.concatenate([gate_mat[:, even:], up_mat[:, even:]], axis=1)
            last = jnp.dot(rows, both, preferred_element_type=F32)
            gate = jnp.concatenate([gate, last[:, :rest]], axis=1)
            upper = jnp.concatenate([upper, last[:, rest:]], axis=1)
        inners.append((gate * jax.nn.sigmoid(gate) * upper * share).astype(BF16))
    inner = jnp.concatenate(inners, axis=1)
    down = jnp.concatenate([down_ref[0, 0], down_ref[0, 1]], axis=0)
    answer = jnp.dot(inner, down, preferred_element_type=F32)
    split = kept_ref.shape[0]
    kept_ref[...] = answer[:split]
    sent_ref[...] = answer[split:].astype(BF16)


def expert_sums(own, sibling, w_gate, w_up, w_down):
    local_rows = own[0].shape[0]
    width = w_down.shape[3]
    rows = local_rows * len(own)
    vmem = pl.BlockSpec(memory_space=pltpu.VMEM)
    weight_count = 2 * 3 * w_down.shape[2] * width
    return pl.pallas_call(
        expert_kernel,
        out_shape=(
            jax.ShapeDtypeStruct((rows, width), F32),
            jax.ShapeDtypeStruct((rows, width), BF16),
        ),
        in_specs=[vmem] * (2 * len(own) + 3),
        out_specs=(vmem, vmem),
        compiler_params=pltpu.CompilerParams(vmem_limit_bytes=24 * 2**20),
        cost_estimate=pl.CostEstimate(
            flops=2 * 2 * rows * weight_count,
            bytes_accessed=2 * weight_count,
            transcendentals=0,
        ),
        name="experts",
    )(*own, *sibling, w_gate, w_up, w_down)


def dense(residual, norm_gain, expert_ids, route_weights, w_gate, w_up, w_down):
    rows = residual.shape[0]
    far = lax.axis_size("ep") // 2
    near, left, both = far // 2, far // 4, far // 2 + far // 4

    def to(value, mask):
        return exchanged(value, "ep", mask)

    def widened(value, mask):
        return to(value.astype(BF16), mask).astype(F32)

    gap()
    own = outgoing_message(residual, norm_gain, expert_ids, route_weights)
    from_far = to(own, far)
    from_left = to(own, left)
    near_half = {"own": own, "left": from_left, "near": to(own, near), "both": to(from_left, near)}
    far_half = {
        "far": from_far,
        "far_both": to(from_far, both),
        "far_left": to(from_far, left),
        "far_near": to(from_far, near),
    }

    def answers(blocks):
        sibling = [to(block, 1) for block in blocks.values()]
        kept, sent = expert_sums(list(blocks.values()), sibling, w_gate, w_up, w_down)
        return kept, to(sent, 1)

    def split(kept, back, names):
        total = kept + back.astype(F32)
        return {name: total[i * rows : (i + 1) * rows] for i, name in enumerate(names)}

    kept_near_half, back_near_half = answers(near_half)
    kept_far_half, back_far_half = answers(far_half)
    kept_far_half, back_far_half, kept_near_half = lax.optimization_barrier(
        (kept_far_half, back_far_half, kept_near_half)
    )
    total = split(kept_near_half, back_near_half, near_half)
    total.update(split(kept_far_half, back_far_half, far_half))

    beside = widened(total["left"], left)
    by_both = widened(total["far_both"], both)
    by_left = widened(total["far_left"], left)
    by_near = widened(total["far_near"], near)
    below = widened(total["near"], near)
    across = widened(total["both"], both)
    opposite = widened(total["far"] + by_left + by_near + by_both, far)
    combined = total["own"] + beside + below + across + opposite
    return (residual.astype(F32) + combined).astype(BF16)


def half_ffn(inputs, gate_mat, up_mat, down_mat):
    gate_part = jnp.dot(inputs, gate_mat, preferred_element_type=jnp.float32)
    upper = jnp.dot(inputs, up_mat, preferred_element_type=jnp.float32)
    inner = (jax.nn.silu(gate_part) * upper).astype(jnp.bfloat16)
    return jnp.dot(inner, down_mat, preferred_element_type=jnp.float32)


def pair_tables(expert_ids, shares, normed, block_total, slot_total):
    local_rows = normed.shape[0]
    expert_total = 2 * block_total
    block_iota = lax.broadcasted_iota(jnp.int32, (1, 1, block_total), 2)
    block_hits = jnp.any((expert_ids // 2)[:, :, None] == block_iota, axis=1).astype(jnp.int32)
    block_rank = jnp.cumsum(block_hits, axis=0) - 1
    hit_wide = jnp.repeat(block_hits, slot_total, axis=1)
    rank_wide = jnp.repeat(block_rank, slot_total, axis=1)
    slot_place = lax.broadcasted_iota(jnp.int32, (1, block_total * slot_total), 1) % slot_total
    picker = jnp.logical_and(hit_wide > 0, rank_wide == slot_place)
    expert_iota = lax.broadcasted_iota(jnp.int32, (1, 1, expert_total), 2)
    expert_mask = expert_ids[:, :, None] == expert_iota
    share_table = jnp.sum(
        jnp.where(expert_mask, shares[:, :, None], jnp.zeros((), jnp.bfloat16)), axis=1
    )
    share_wide = jnp.repeat(share_table.reshape(local_rows, block_total, 2), slot_total, axis=1)
    slot_weights = jnp.sum(
        jnp.where(picker[:, :, None], share_wide, jnp.zeros((), jnp.bfloat16)), axis=0
    )
    slot_rows = jnp.einsum(
        "rs,rd->sd", picker.astype(jnp.bfloat16), normed, preferred_element_type=jnp.float32
    ).astype(jnp.bfloat16)
    return (picker, slot_rows, slot_weights)


def sparse(residual, norm_gain, expert_ids, route_weights, w_gate, w_up, w_down):
    local_rows = residual.shape[0]
    model_width = residual.shape[1]
    widened = residual.astype(jnp.float32)
    scaling = lax.rsqrt(jnp.mean(widened * widened, axis=1, keepdims=True) + 1e-06)
    normed = (widened * scaling * norm_gain.astype(jnp.float32)[None, :]).astype(jnp.bfloat16)
    shares = (route_weights / jnp.sum(route_weights, axis=1, keepdims=True)).astype(jnp.bfloat16)
    device_total = lax.axis_size("ep")
    block_total = device_total // 2
    typical = max(1, local_rows * TOP // device_total)

    def weighted_both(arrived, arrived_weights):
        flat_rows = arrived.reshape(-1, arrived.shape[2])
        flat_weights = arrived_weights.reshape(-1, 2).astype(jnp.float32)
        mixed = flat_weights[:, 0:1] * half_ffn(flat_rows, w_gate[0, 0], w_up[0, 0], w_down[0, 0])
        mixed = mixed + flat_weights[:, 1:2] * half_ffn(
            flat_rows, w_gate[0, 1], w_up[0, 1], w_down[0, 1]
        )
        return mixed.reshape(arrived.shape)

    pair_slots = min(local_rows, 4 * typical)
    half_slots = (pair_slots + 1) // 2
    padded_slots = 2 * half_slots
    picker, slot_rows, slot_weights = pair_tables(
        expert_ids, shares, normed, block_total, padded_slots
    )
    outgoing = slot_rows.reshape(device_total, half_slots, model_width)
    weights_out = slot_weights.reshape(device_total, half_slots, 2)
    arrived = lax.all_to_all(outgoing, "ep", split_axis=0, concat_axis=0, tiled=True)
    arrived_weights = lax.all_to_all(weights_out, "ep", split_axis=0, concat_axis=0, tiled=True)
    other_rows, other_weights = swapped((arrived, arrived_weights), "ep", 0)
    mine = weighted_both(arrived, arrived_weights)
    theirs = weighted_both(other_rows, other_weights)
    back = swapped(theirs, "ep", 0)
    answered = mine + back
    returned = lax.all_to_all(answered, "ep", split_axis=0, concat_axis=0, tiled=True)
    pooled = returned.reshape(block_total * padded_slots, model_width)
    combined = jnp.dot(picker.astype(jnp.float32), pooled, precision=lax.Precision.HIGHEST)
    return (widened + combined).astype(jnp.bfloat16)


def few_experts(devices):
    return devices == 2 * TOP


def local(*args):
    return (dense if few_experts(lax.axis_size("ep")) else sparse)(*args)


def solution(mesh):
    placed = (
        P(("groups", "ep"), None),
        P(),
        P(("groups", "ep"), None),
        P(("groups", "ep"), None),
        P("ep", None, None, None),
        P("ep", None, None, None),
        P("ep", None, None, None),
    )
    return jax.shard_map(
        local, mesh=mesh, in_specs=placed, out_specs=P(("groups", "ep"), None), check_vma=False
    )
```
